512 devices in a mesh: lev: 16 (over x, z_hi, core), hor: 32 (over z_lo, y).
Axes of the slice: x: 4, y: 4, z: 16 (z_hi: 2, z_lo: 8; z = z_hi * 8 + z_lo), core: 2. Of those that a mesh axis runs over, the one named last changes fastest.
Arguments:
- state: float32 [2, 128, 512, 1024], P(None, 'lev', 'hor'), may hold values from -6 to 6
- cotangent: bfloat16 [2, 128, 512, 1024], P(None, 'lev', 'hor'), may hold values from -6 to 6
- diffusion: float32 [128, 512, 1024], P('lev', 'hor'), may hold values from 0.02 to 0.2
- vertical_inverse: float32 [2, 128, 128], replicated, may hold values from -0.2 to 2
- w_in: bfloat16 [1024, 256], replicated, may hold values from -0.375 to 0.375
- w_out: bfloat16 [256, 1024], replicated, may hold values from -0.1875 to 0.1875
Outputs:
- state_adjoint: float32 [2, 128, 512, 1024], P(None, 'lev', 'hor')
The draws below stay inside these ranges and needn't reach their ends.
All inputs are finite; a program needn't handle non-finite values.
Results may differ from the reference program's by a relative error of at most 0.002.
Values may be sent and summed in bfloat16 or wider, within the bound.
A program may use at most 64 MiB of HBM per device.

```python
import math
import jax
import jax.numpy as jnp
from jax import lax

FIELDS = 2
LEV = 128
HID = 1024
NY = 1024
NX = 512
FEAT = 256


def draw_vertical_inverse(key, part):
    key_off = jax.random.fold_in(key, 11)
    key_diag = jax.random.fold_in(key, 23)
    offdiag = jnp.clip(0.05 * jax.random.normal(key_off, (FIELDS, LEV, LEV), jnp.float32), -0.2, 0.2)
    diag_values = jax.random.uniform(key_diag, (FIELDS, LEV), jnp.float32, 1.0, 2.0)
    identity = jnp.eye(LEV, dtype=jnp.float32)
    return offdiag * (1.0 - identity) + identity * diag_values[:, :, None]


def steps_of(key, extent, cuts, low, top_value):
    def one(axis_at, parts):
        draws = jax.random.uniform(jax.random.fold_in(jax.random.fold_in(key, 6), axis_at), (parts,), jnp.float32, low / len(cuts), top_value / len(cuts))
        return jnp.repeat(jnp.exp(draws), extent[axis_at] // parts).reshape((-1,) + (1,) * (len(extent) - axis_at - 1))

    factor_of = one(*cuts[0])
    for cut in cuts[1:]:
        factor_of = factor_of * one(*cut)
    return factor_of


def gaussian(key, extent, deviation, bound, cuts=(), held_as=jnp.bfloat16):
    drawn = jax.random.normal(key, extent, jnp.float32) * deviation
    if len(cuts) > 0:
        drawn = steps_of(key, extent, cuts, -0.22, 0.18) * drawn
    return jnp.clip(drawn, min=-bound, max=bound).astype(held_as)


def setup_inputs(seed: int = 0) -> dict:
    streams_of = jax.random.split(jax.random.key(seed), 7)
    state = gaussian(streams_of[0], (FIELDS, LEV, NX, NY), 1.0, 6.0, ((1, 16), (2, 32)), jnp.float32)
    cotangent = gaussian(streams_of[1], (FIELDS, LEV, NX, NY), 1.0, 6.0, ((1, 16), (2, 32)))
    diffusion = jnp.clip(jnp.exp(math.log(0.2) - 2.3025851 * jax.random.uniform(streams_of[2], (LEV, NX, NY), jnp.float32) ** steps_of(streams_of[2], (LEV, NX, NY), ((0, 16), (1, 32)), -0.2, 0.2)), 0.02, 0.2)
    vertical_inverse = draw_vertical_inverse(jax.random.fold_in(streams_of[6], 71), 0)
    w_in = gaussian(streams_of[4], (HID, FEAT), FEAT ** -0.5, 0.375)
    w_out = gaussian(streams_of[5], (FEAT, HID), HID ** -0.5, 0.1875)
    return {"state": state, "cotangent": cotangent, "diffusion": diffusion, "vertical_inverse": vertical_inverse, "w_in": w_in, "w_out": w_out}


def laplace(field):
    padded = jnp.pad(field, ((0, 0), (0, 0), (1, 1), (1, 1)))
    return (padded[:, :, 2:, 1:-1] + padded[:, :, :-2, 1:-1] + padded[:, :, 1:-1, 2:]
            + padded[:, :, 1:-1, :-2] - 4.0 * padded[:, :, 1:-1, 1:-1])


def column_adjoint(diffused, cot_block, vertical_inverse, w_in, w_out):
    highest = lax.Precision.HIGHEST
    solved = jnp.einsum("fkl,flc->fkc", vertical_inverse, diffused, precision=highest)
    fields, levels, count = solved.shape
    inputs = solved.reshape(fields * levels, count).astype(jnp.bfloat16)
    preact = jnp.dot(w_in, inputs, preferred_element_type=jnp.float32)
    cot_cols = cot_block.reshape(fields * levels, count)
    hidden_grad = lax.dot_general(w_out, cot_cols, (((0,), (0,)), ((), ())), preferred_element_type=jnp.float32)
    squashed = jax.nn.sigmoid(preact)
    pre_grad = (hidden_grad * squashed * (1.0 + preact * (1.0 - squashed))).astype(jnp.bfloat16)
    level_grad = cot_cols.astype(jnp.float32) + lax.dot_general(w_in, pre_grad, (((0,), (0,)), ((), ())), preferred_element_type=jnp.float32)
    level_grad = level_grad.reshape(fields, levels, count)
    return jnp.einsum("fkl,fkc->flc", vertical_inverse, level_grad, precision=highest)


def reference(state, cotangent, diffusion, vertical_inverse, w_in, w_out):
    diffused = state + diffusion[None] * laplace(state)
    rows_first = jnp.moveaxis(diffused, 2, 0)
    cot_first = jnp.moveaxis(cotangent, 2, 0)

    def one_row(pair):
        return column_adjoint(pair[0], pair[1], vertical_inverse, w_in, w_out)

    adjoint_rows = lax.map(one_row, (rows_first, cot_first))
    adjoint_diffused = jnp.moveaxis(adjoint_rows, 0, 2)
    return adjoint_diffused + laplace(diffusion[None] * adjoint_diffused)
```

```python
import functools

import jax
import jax.numpy as jnp
from jax import lax
from jax.experimental import pallas as pl
from jax.experimental.pallas import tpu as pltpu
from jax.sharding import PartitionSpec as P

MESH = pl.DeviceIdType.MESH
F32 = jnp.float32
BF16 = jnp.bfloat16
CHUNKS = 4
COLS = 1024
WIDE = COLS // CHUNKS
LEVS = 16
ROWS = 16
HID = 1024
TILES = COLS // 128


def nt(a, b):
    return lax.dot_general(a, b, (((1,), (1,)), ((), ())), preferred_element_type=F32)


def nn(a, b):
    return jnp.dot(a, b, preferred_element_type=F32)


def sides_of(block):
    lane = lax.broadcasted_iota(jnp.int32, block.shape, 1)
    left = jnp.where(lane == 0, 0.0, pltpu.roll(block, 1, 1))
    right = jnp.where(lane == block.shape[1] - 1, 0.0, pltpu.roll(block, block.shape[1] - 1, 1))
    return left + right


def kernel(
    state_hbm, cot_hbm, diff_hbm, vinv_hbm, w_in_hbm, w_out_hbm, out_hbm,
    state_v, cot_v, diff_v, vinv_v, w_in_v, w_out_v, out_v,
    cot_f, grid_s, grid_w, adj_v,
    s_cot, r_cot, s_state, r_state, s_adj, r_adj,
    w_in_p, w_in_t, w_out_t, v_fwd, v_adj, gain,
    in_sems, tile_sems, cot_sems, state_sems, adj_sems, halo_a, halo_b,
):
    me = lax.axis_index("lev")
    hor = lax.axis_index("hor")
    last = lax.axis_size("hor") - 1

    def tiles(wide, tall, sem, out=False):
        pairs = [(wide.at[:, pl.ds(t * 128, 128)], tall.at[t]) for t in range(TILES)]
        return [pltpu.make_async_copy(b, a, sem.at[t]) if out else pltpu.make_async_copy(a, b, sem.at[t])
                for t, (a, b) in enumerate(pairs)]

    cot_load = pltpu.make_async_copy(cot_hbm, cot_v, in_sems.at[0])
    state_load = tiles(state_hbm, state_v, tile_sems.at[0])
    rest = tiles(diff_hbm, diff_v, tile_sems.at[1]) + [
        pltpu.make_async_copy(src, dst, in_sems.at[i + 1])
        for i, (src, dst) in enumerate(((vinv_hbm, vinv_v), (w_in_hbm, w_in_v), (w_out_hbm, w_out_v)))
    ]
    loads = [cot_load] + state_load + rest
    for load in loads:
        load.start()

    barrier = pltpu.get_barrier_semaphore()

    @pl.loop(1, LEVS)
    def _(j):
        pl.semaphore_signal(
            barrier, inc=1, device_id={"lev": lax.rem(me + j, LEVS), "hor": hor}, device_id_type=MESH
        )

    @pl.when(hor > 0)
    def _():
        pl.semaphore_signal(barrier, inc=1, device_id={"lev": me, "hor": hor - 1}, device_id_type=MESH)

    @pl.when(hor < last)
    def _():
        pl.semaphore_signal(barrier, inc=1, device_id={"lev": me, "hor": hor + 1}, device_id_type=MESH)

    def across(ref, base, lo=0, hi=COLS):
        return jnp.concatenate(
            [ref[t, pl.ds(base, 8, stride=ROWS), :] for t in range(lo // 128, hi // 128)], axis=1
        )

    def both(ref, r):
        return jnp.concatenate([across(ref, r), across(ref, 128 + r)], axis=0)

    def doubled(ref, r, lo=0, hi=COLS):
        coef = across(ref, r, lo, hi)
        return jnp.concatenate([coef, coef], axis=0)

    cot_load.wait()
    for t in range(TILES):
        cot_f[t] = cot_v[:, t * 128:(t + 1) * 128].astype(F32)

    @pl.loop(0, ROWS)
    def _(r):
        row = both(cot_f, r).astype(BF16)
        for c in range(CHUNKS):
            s_cot[c, r] = row[:, c * WIDE:(c + 1) * WIDE]

    for c in range(CHUNKS):
        r_cot[c, me] = s_cot[c, me]

    for load in state_load:
        load.wait()

    @pl.loop(0, ROWS)
    def _(r):
        grid_s[r + 1] = both(state_v, r)

    @pl.when(hor == 0)
    def _():
        grid_s[0] = jnp.zeros((16, COLS), F32)
        grid_w[0] = jnp.zeros((16, COLS), F32)

    @pl.when(hor == last)
    def _():
        grid_s[ROWS + 1] = jnp.zeros((16, COLS), F32)
        grid_w[ROWS + 1] = jnp.zeros((16, COLS), F32)

    for load in rest:
        load.wait()

    pl.semaphore_wait(
        barrier, LEVS - 1 + (hor > 0).astype(jnp.int32) + (hor < last).astype(jnp.int32)
    )

    def edge(grid, sems, up, cols):
        src, dst = (ROWS, 0) if up else (1, ROWS + 1)
        return pltpu.make_async_remote_copy(
            src_ref=grid.at[src, :, cols], dst_ref=grid.at[dst, :, cols],
            send_sem=sems.at[0, int(up)], recv_sem=sems.at[1, int(up)],
            device_id={"lev": me, "hor": hor + (1 if up else -1)}, device_id_type=MESH,
        )

    def swap_start(grid, sems, cols):
        @pl.when(hor > 0)
        def _():
            edge(grid, sems, False, cols).start()

        @pl.when(hor < last)
        def _():
            edge(grid, sems, True, cols).start()

    def swap_wait(grid, sems, cols):
        @pl.when(hor > 0)
        def _():
            edge(grid, sems, False, cols).wait_send()
            edge(grid, sems, True, cols).wait_recv()

        @pl.when(hor < last)
        def _():
            edge(grid, sems, True, cols).wait_send()
            edge(grid, sems, False, cols).wait_recv()

    def spread(src, dst, sems, c):
        @pl.loop(1, LEVS)
        def _(j):
            peer = lax.rem(me + j, LEVS)
            pltpu.make_async_remote_copy(
                src_ref=src.at[c, peer], dst_ref=dst.at[c, me],
                send_sem=sems.at[0, c], recv_sem=sems.at[1, c],
                device_id={"lev": peer, "hor": hor}, device_id_type=MESH,
            ).start()

    def gathered(buf, sems, way, c):
        part = buf.at[c, pl.ds(0, LEVS - 1)]
        pltpu.make_async_copy(part, part, sems.at[way, c]).wait()

    full = pl.ds(0, COLS)
    swap_start(grid_s, halo_a, full)
    for c in range(CHUNKS):
        spread(s_cot, r_cot, cot_sems, c)

    swap_wait(grid_s, halo_a, full)

    @pl.loop(0, ROWS)
    def _(r):
        mid = grid_s[r + 1]
        around = grid_s[r] + grid_s[r + 2] + sides_of(mid) - 4.0 * mid
        row = (mid + doubled(diff_v, r) * around).astype(BF16)
        for c in range(CHUNKS):
            s_state[c, r] = row[:, c * WIDE:(c + 1) * WIDE]

    for c in range(CHUNKS):
        spread(s_state, r_state, state_sems, c)
    for c in range(CHUNKS):
        r_state[c, me] = s_state[c, me]

    at_p = lax.broadcasted_iota(jnp.int32, (256, 256), 0)
    at_k = lax.broadcasted_iota(jnp.int32, (256, 256), 1)
    place = (at_p // 16) * 8 + (at_p % 16) // 8 * 128 + at_p % 8
    perm_t = (place == at_k).astype(F32).astype(BF16)
    w_in_p[...] = nt(w_in_v[...], perm_t).astype(BF16)
    w_in_t[...] = nt(perm_t, w_in_v[...]).astype(BF16)
    w_out_t[...] = nn(perm_t, w_out_v[...]).T.astype(BF16)
    eye = lax.broadcasted_iota(jnp.int32, (128, 128), 0) == lax.broadcasted_iota(jnp.int32, (128, 128), 1)
    parts = [jnp.zeros((256, 256), F32) for _ in range(2)]
    for f in range(2):
        exact = vinv_v[f]
        high = exact.astype(BF16)
        low = (exact - high.astype(F32)).astype(BF16)
        sel = perm_t[:, f * 128:(f + 1) * 128]
        for i, piece in enumerate((high, low)):
            parts[i] += nn(sel, nt(piece, sel).astype(BF16))
        diag = jnp.sum(jnp.where(eye, exact, 0.0), axis=1, keepdims=True)
        for src in range(LEVS):
            gain[src * 16 + f * 8:src * 16 + f * 8 + 8, :] = jnp.broadcast_to(
                diag[src * 8:src * 8 + 8], (8, 128)
            )
    for i in range(2):
        v_fwd[:, i * 256:(i + 1) * 256] = parts[i].astype(BF16)
    high_t = parts[0].T.astype(BF16)
    v_adj[:, 0:256] = high_t
    v_adj[:, 256:512] = high_t
    v_adj[:, 512:768] = parts[1].T.astype(BF16)

    def columns(c):
        diffused = r_state[c].reshape(256, WIDE)
        cot = r_cot[c].reshape(256, WIDE)
        solved = nn(v_fwd[...], jnp.concatenate([diffused, diffused], axis=0))
        inputs = solved.astype(BF16)
        level = cot.astype(F32)
        for h in range(4):
            hs = slice(h * 256, (h + 1) * 256)
            preact = nn(w_in_p[hs, :], inputs)
            hidden = nn(w_out_t[hs, :], cot)
            s = 0.5 + 0.5 * jnp.tanh(0.5 * preact)
            pre = (hidden * s * (1.0 + preact * (1.0 - s))).astype(BF16)
            level = level + nn(w_in_t[:, hs], pre)
        high = level.astype(BF16)
        low = (level - high.astype(F32)).astype(BF16)
        adjoint = nn(v_adj[...], jnp.concatenate([high, low, high], axis=0))
        delta = adjoint - gain[:, 0:1] * cot.astype(F32)
        s_adj[c] = delta.astype(BF16).reshape(LEVS, 16, WIDE)

    @pl.loop(0, CHUNKS)
    def _(c):
        gathered(r_cot, cot_sems, 1, c)
        gathered(r_state, state_sems, 1, c)
        columns(c)
        spread(s_adj, r_adj, adj_sems, c)
        r_adj[c, me] = s_adj[c, me]

    scale = gain[pl.ds(pl.multiple_of(me * 16, 16), 16), 0:1]
    for c in range(CHUNKS):
        gathered(r_adj, adj_sems, 1, c)
        cols = slice(c * WIDE, (c + 1) * WIDE)

        @pl.loop(0, ROWS)
        def _(r):
            adj = r_adj[c, r].astype(F32) + scale * s_cot[c, r].astype(F32)
            adj_v[r, :, cols] = adj
            grid_w[r + 1, :, cols] = doubled(diff_v, r, c * WIDE, (c + 1) * WIDE) * adj

        swap_start(grid_w, halo_b.at[c], pl.ds(c * WIDE, WIDE))
    for c in range(CHUNKS):
        swap_wait(grid_w, halo_b.at[c], pl.ds(c * WIDE, WIDE))

    @pl.loop(0, ROWS)
    def _(r):
        mid = grid_w[r + 1]
        row = adj_v[r] + (grid_w[r] + grid_w[r + 2] + sides_of(mid) - 4.0 * mid)
        for t in range(TILES):
            out_v[t, pl.ds(r, 8, stride=ROWS), :] = row[0:8, t * 128:(t + 1) * 128]
            out_v[t, pl.ds(128 + r, 8, stride=ROWS), :] = row[8:16, t * 128:(t + 1) * 128]

    stores = tiles(out_hbm, out_v, tile_sems.at[2], out=True)
    for store in stores:
        store.start()
    for c in range(CHUNKS):
        gathered(s_cot, cot_sems, 0, c)
        gathered(s_state, state_sems, 0, c)
        gathered(s_adj, adj_sems, 0, c)
    for store in stores:
        store.wait()


def body(state, cotangent, diffusion, vertical_inverse, w_in, w_out):
    dma = pltpu.SemaphoreType.DMA
    slabs = (CHUNKS, LEVS, 16, WIDE)
    out = pl.pallas_call(
        kernel,
        out_shape=jax.ShapeDtypeStruct((256, COLS), F32),
        in_specs=[pl.BlockSpec(memory_space=pltpu.HBM)] * 6,
        out_specs=pl.BlockSpec(memory_space=pl.ANY),
        scratch_shapes=[
            pltpu.VMEM((TILES, 256, 128), F32), pltpu.VMEM((256, COLS), BF16), pltpu.VMEM((TILES, 128, 128), F32),
            pltpu.VMEM((2, 128, 128), F32), pltpu.VMEM((HID, 256), BF16), pltpu.VMEM((256, HID), BF16),
            pltpu.VMEM((TILES, 256, 128), F32),
            pltpu.VMEM((TILES, 256, 128), F32), pltpu.VMEM((ROWS + 2, 16, COLS), F32),
            pltpu.VMEM((ROWS + 2, 16, COLS), F32), pltpu.VMEM((ROWS, 16, COLS), F32),
        ] + [pltpu.VMEM(slabs, BF16)] * 6 + [
            pltpu.VMEM((HID, 256), BF16), pltpu.VMEM((256, HID), BF16), pltpu.VMEM((HID, 256), BF16),
            pltpu.VMEM((256, 512), BF16), pltpu.VMEM((256, 768), BF16), pltpu.VMEM((256, 128), F32),
            dma((4,)), dma((3, TILES)), dma((2, CHUNKS)), dma((2, CHUNKS)), dma((2, CHUNKS)), dma((2, 2)), dma((CHUNKS, 2, 2)),
        ],
        compiler_params=pltpu.CompilerParams(
            collective_id=0, has_side_effects=True, vmem_limit_bytes=48 << 20
        ),
    )(
        state.reshape(256, COLS), cotangent.reshape(256, COLS), diffusion.reshape(128, COLS),
        vertical_inverse, w_in, w_out,
    )
    return out.reshape(2, 8, ROWS, COLS)


def solution(mesh):
    placed = (
        P(None, "lev", "hor", None),
        P(None, "lev", "hor", None),
        P("lev", "hor", None),
        P(),
        P(),
        P(),
    )
    return jax.shard_map(
        body, mesh=mesh, in_specs=placed, out_specs=P(None, "lev", "hor", None), check_vma=False
    )
```

```python
import functools

import jax
import jax.numpy as jnp
from jax import lax
from jax.experimental import pallas as pl
from jax.experimental.pallas import tpu as pltpu
from jax.sharding import PartitionSpec as P

MESH = pl.DeviceIdType.MESH
F32 = jnp.float32
BF16 = jnp.bfloat16
CHUNKS = 4
COLS = 1024
WIDE = COLS // CHUNKS
LEVS = 16
ROWS = 16
HID = 1024
TILES = COLS // 128


def nt(a, b):
    return lax.dot_general(a, b, (((1,), (1,)), ((), ())), preferred_element_type=F32)


def nn(a, b):
    return jnp.dot(a, b, preferred_element_type=F32)


def sides_of(block):
    lane = lax.broadcasted_iota(jnp.int32, block.shape, 1)
    left = jnp.where(lane == 0, 0.0, pltpu.roll(block, 1, 1))
    right = jnp.where(lane == block.shape[1] - 1, 0.0, pltpu.roll(block, block.shape[1] - 1, 1))
    return left + right


def kernel(
    state_hbm, cot_hbm, diff_hbm, vinv_hbm, w_in_hbm, w_out_hbm, out_hbm,
    state_v, cot_v, diff_v, vinv_v, w_in_v, w_out_v, out_v,
    cot_f, grid_s, grid_w, adj_v,
    s_cot, r_cot, s_state, r_state, s_adj, r_adj,
    w_in_p, w_in_t, w_out_t, v_fwd, v_adj, gain,
    in_sems, tile_sems, cot_sems, state_sems, adj_sems, halo_a, halo_b,
):
    me = lax.axis_index("lev")
    hor = lax.axis_index("hor")
    last = lax.axis_size("hor") - 1

    def tiles(wide, tall, sem, out=False):
        pairs = [(wide.at[:, pl.ds(t * 128, 128)], tall.at[t]) for t in range(TILES)]
        return [pltpu.make_async_copy(b, a, sem.at[t]) if out else pltpu.make_async_copy(a, b, sem.at[t])
                for t, (a, b) in enumerate(pairs)]

    cot_load = pltpu.make_async_copy(cot_hbm, cot_v, in_sems.at[0])
    state_load = tiles(state_hbm, state_v, tile_sems.at[0])
    rest = tiles(diff_hbm, diff_v, tile_sems.at[1]) + [
        pltpu.make_async_copy(src, dst, in_sems.at[i + 1])
        for i, (src, dst) in enumerate(((vinv_hbm, vinv_v), (w_in_hbm, w_in_v), (w_out_hbm, w_out_v)))
    ]
    loads = [cot_load] + state_load + rest
    for load in loads:
        load.start()

    barrier = pltpu.get_barrier_semaphore()

    @pl.loop(1, LEVS)
    def _(j):
        pl.semaphore_signal(
            barrier, inc=1, device_id={"lev": lax.rem(me + j, LEVS), "hor": hor}, device_id_type=MESH
        )

    @pl.when(hor > 0)
    def _():
        pl.semaphore_signal(barrier, inc=1, device_id={"lev": me, "hor": hor - 1}, device_id_type=MESH)

    @pl.when(hor < last)
    def _():
        pl.semaphore_signal(barrier, inc=1, device_id={"lev": me, "hor": hor + 1}, device_id_type=MESH)

    def across(ref, base, lo=0, hi=COLS):
        return jnp.concatenate(
            [ref[t, pl.ds(base, 8, stride=ROWS), :] for t in range(lo // 128, hi // 128)], axis=1
        )

    def both(ref, r):
        return jnp.concatenate([across(ref, r), across(ref, 128 + r)], axis=0)

    def doubled(ref, r, lo=0, hi=COLS):
        coef = across(ref, r, lo, hi)
        return jnp.concatenate([coef, coef], axis=0)

    cot_load.wait()
    for t in range(TILES):
        cot_f[t] = cot_v[:, t * 128:(t + 1) * 128].astype(F32)

    @pl.loop(0, ROWS)
    def _(r):
        row = both(cot_f, r).astype(BF16)
        for c in range(CHUNKS):
            s_cot[c, r] = row[:, c * WIDE:(c + 1) * WIDE]

    for c in range(CHUNKS):
        r_cot[c, me] = s_cot[c, me]

    for load in state_load:
        load.wait()

    @pl.loop(0, ROWS)
    def _(r):
        grid_s[r + 1] = both(state_v, r)

    @pl.when(hor == 0)
    def _():
        grid_s[0] = jnp.zeros((16, COLS), F32)
        grid_w[0] = jnp.zeros((16, COLS), F32)

    @pl.when(hor == last)
    def _():
        grid_s[ROWS + 1] = jnp.zeros((16, COLS), F32)
        grid_w[ROWS + 1] = jnp.zeros((16, COLS), F32)

    for load in rest:
        load.wait()

    pl.semaphore_wait(
        barrier, LEVS - 1 + (hor > 0).astype(jnp.int32) + (hor < last).astype(jnp.int32)
    )

    def edge(grid, sems, up, cols):
        src, dst = (ROWS, 0) if up else (1, ROWS + 1)
        return pltpu.make_async_remote_copy(
            src_ref=grid.at[src, :, cols], dst_ref=grid.at[dst, :, cols],
            send_sem=sems.at[0, int(up)], recv_sem=sems.at[1, int(up)],
            device_id={"lev": me, "hor": hor + (1 if up else -1)}, device_id_type=MESH,
        )

    def swap_start(grid, sems, cols):
        @pl.when(hor > 0)
        def _():
            edge(grid, sems, False, cols).start()

        @pl.when(hor < last)
        def _():
            edge(grid, sems, True, cols).start()

    def swap_wait(grid, sems, cols):
        @pl.when(hor > 0)
        def _():
            edge(grid, sems, False, cols).wait_send()
            edge(grid, sems, True, cols).wait_recv()

        @pl.when(hor < last)
        def _():
            edge(grid, sems, True, cols).wait_send()
            edge(grid, sems, False, cols).wait_recv()

    def spread(src, dst, sems, c):
        @pl.loop(1, LEVS)
        def _(j):
            peer = lax.rem(me + j, LEVS)
            pltpu.make_async_remote_copy(
                src_ref=src.at[c, peer], dst_ref=dst.at[c, me],
                send_sem=sems.at[0, c], recv_sem=sems.at[1, c],
                device_id={"lev": peer, "hor": hor}, device_id_type=MESH,
            ).start()

    def gathered(buf, sems, way, c):
        part = buf.at[c, pl.ds(0, LEVS - 1)]
        pltpu.make_async_copy(part, part, sems.at[way, c]).wait()

    full = pl.ds(0, COLS)
    swap_start(grid_s, halo_a, full)
    for c in range(CHUNKS):
        spread(s_cot, r_cot, cot_sems, c)

    swap_wait(grid_s, halo_a, full)

    @pl.loop(0, ROWS)
    def _(r):
        mid = grid_s[r + 1]
        around = grid_s[r] + grid_s[r + 2] + sides_of(mid) - 4.0 * mid
        row = (mid + doubled(diff_v, r) * around).astype(BF16)
        for c in range(CHUNKS):
            s_state[c, r] = row[:, c * WIDE:(c + 1) * WIDE]

    for c in range(CHUNKS):
        spread(s_state, r_state, state_sems, c)
    for c in range(CHUNKS):
        r_state[c, me] = s_state[c, me]

    at_p = lax.broadcasted_iota(jnp.int32, (256, 256), 0)
    at_k = lax.broadcasted_iota(jnp.int32, (256, 256), 1)
    place = (at_p // 16) * 8 + (at_p % 16) // 8 * 128 + at_p % 8
    perm_t = (place == at_k).astype(F32).astype(BF16)
    w_in_p[...] = nt(w_in_v[...], perm_t).astype(BF16)
    w_in_t[...] = nt(perm_t, w_in_v[...]).astype(BF16)
    w_out_t[...] = nn(perm_t, w_out_v[...]).T.astype(BF16)
    eye = lax.broadcasted_iota(jnp.int32, (128, 128), 0) == lax.broadcasted_iota(jnp.int32, (128, 128), 1)
    parts = [jnp.zeros((256, 256), F32) for _ in range(2)]
    for f in range(2):
        exact = vinv_v[f]
        high = exact.astype(BF16)
        low = (exact - high.astype(F32)).astype(BF16)
        sel = perm_t[:, f * 128:(f + 1) * 128]
        for i, piece in enumerate((high, low)):
            parts[i] += nn(sel, nt(piece, sel).astype(BF16))
        diag = jnp.sum(jnp.where(eye, exact, 0.0), axis=1, keepdims=True)
        for src in range(LEVS):
            gain[src * 16 + f * 8:src * 16 + f * 8 + 8, :] = jnp.broadcast_to(
                diag[src * 8:src * 8 + 8], (8, 128)
            )
    for i in range(2):
        v_fwd[:, i * 256:(i + 1) * 256] = parts[i].astype(BF16)
    high_t = parts[0].T.astype(BF16)
    v_adj[:, 0:256] = high_t
    v_adj[:, 256:512] = high_t
    v_adj[:, 512:768] = parts[1].T.astype(BF16)

    def columns(c):
        diffused = r_state[c].reshape(256, WIDE)
        cot = r_cot[c].reshape(256, WIDE)
        solved = nn(v_fwd[...], jnp.concatenate([diffused, diffused], axis=0))
        inputs = solved.astype(BF16)
        level = cot.astype(F32)
        for h in range(4):
            hs = slice(h * 256, (h + 1) * 256)
            preact = nn(w_in_p[hs, :], inputs)
            hidden = nn(w_out_t[hs, :], cot)
            s = 0.5 + 0.5 * jnp.tanh(0.5 * preact)
            pre = (hidden * s * (1.0 + preact * (1.0 - s))).astype(BF16)
            level = level + nn(w_in_t[:, hs], pre)
        high = level.astype(BF16)
        low = (level - high.astype(F32)).astype(BF16)
        adjoint = nn(v_adj[...], jnp.concatenate([high, low, high], axis=0))
        delta = adjoint - gain[:, 0:1] * cot.astype(F32)
        s_adj[c] = delta.astype(BF16).reshape(LEVS, 16, WIDE)

    @pl.loop(0, CHUNKS)
    def _(c):
        gathered(r_cot, cot_sems, 1, c)
        gathered(r_state, state_sems, 1, c)
        columns(c)
        spread(s_adj, r_adj, adj_sems, c)
        r_adj[c, me] = s_adj[c, me]

    scale = gain[pl.ds(pl.multiple_of(me * 16, 16), 16), 0:1]
    for c in range(CHUNKS):
        gathered(r_adj, adj_sems, 1, c)
        cols = slice(c * WIDE, (c + 1) * WIDE)

        @pl.loop(0, ROWS)
        def _(r):
            adj = r_adj[c, r].astype(F32) + scale * s_cot[c, r].astype(F32)
            adj_v[r, :, cols] = adj
            grid_w[r + 1, :, cols] = doubled(diff_v, r, c * WIDE, (c + 1) * WIDE) * adj

        swap_start(grid_w, halo_b.at[c], pl.ds(c * WIDE, WIDE))
    for c in range(CHUNKS):
        swap_wait(grid_w, halo_b.at[c], pl.ds(c * WIDE, WIDE))

    @pl.loop(0, ROWS)
    def _(r):
        mid = grid_w[r + 1]
        row = adj_v[r] + (grid_w[r] + grid_w[r + 2] + sides_of(mid) - 4.0 * mid)
        for t in range(TILES):
            out_v[t, pl.ds(r, 8, stride=ROWS), :] = row[0:8, t * 128:(t + 1) * 128]
            out_v[t, pl.ds(128 + r, 8, stride=ROWS), :] = row[8:16, t * 128:(t + 1) * 128]

    stores = tiles(out_hbm, out_v, tile_sems.at[2], out=True)
    for store in stores:
        store.start()
    for c in range(CHUNKS):
        gathered(s_cot, cot_sems, 0, c)
        gathered(s_state, state_sems, 0, c)
        gathered(s_adj, adj_sems, 0, c)
    for store in stores:
        store.wait()


def body(state, cotangent, diffusion, vertical_inverse, w_in, w_out):
    dma = pltpu.SemaphoreType.DMA
    slabs = (CHUNKS, LEVS, 16, WIDE)
    out = pl.pallas_call(
        kernel,
        out_shape=pltpu.VMEM((256, COLS), F32),
        in_specs=[pl.BlockSpec(memory_space=pltpu.HBM)] * 6,
        out_specs=pl.BlockSpec(memory_space=pltpu.VMEM),
        scratch_shapes=[
            pltpu.VMEM((TILES, 256, 128), F32), pltpu.VMEM((256, COLS), BF16), pltpu.VMEM((TILES, 128, 128), F32),
            pltpu.VMEM((2, 128, 128), F32), pltpu.VMEM((HID, 256), BF16), pltpu.VMEM((256, HID), BF16),
            pltpu.VMEM((TILES, 256, 128), F32),
            pltpu.VMEM((TILES, 256, 128), F32), pltpu.VMEM((ROWS + 2, 16, COLS), F32),
            pltpu.VMEM((ROWS + 2, 16, COLS), F32), pltpu.VMEM((ROWS, 16, COLS), F32),
        ] + [pltpu.VMEM(slabs, BF16)] * 6 + [
            pltpu.VMEM((HID, 256), BF16), pltpu.VMEM((256, HID), BF16), pltpu.VMEM((HID, 256), BF16),
            pltpu.VMEM((256, 512), BF16), pltpu.VMEM((256, 768), BF16), pltpu.VMEM((256, 128), F32),
            dma((4,)), dma((3, TILES)), dma((2, CHUNKS)), dma((2, CHUNKS)), dma((2, CHUNKS)), dma((2, 2)), dma((CHUNKS, 2, 2)),
        ],
        compiler_params=pltpu.CompilerParams(
            collective_id=0, has_side_effects=True, vmem_limit_bytes=44 << 20
        ),
    )(*[
        pltpu.with_memory_space_constraint(x, pltpu.HBM)
        for x in (state.reshape(256, COLS), cotangent.reshape(256, COLS), diffusion.reshape(128, COLS),
                  vertical_inverse, w_in, w_out)
    ])
    return out.reshape(2, 8, ROWS, COLS)


def solution(mesh):
    placed = (
        P(None, "lev", "hor", None),
        P(None, "lev", "hor", None),
        P("lev", "hor", None),
        P(),
        P(),
        P(),
    )
    return jax.shard_map(
        body, mesh=mesh, in_specs=placed, out_specs=P(None, "lev", "hor", None), check_vma=False
    )
```

```python
import functools

import jax
import jax.numpy as jnp
from jax import lax
from jax.experimental import pallas as pl
from jax.experimental.pallas import tpu as pltpu
from jax.sharding import PartitionSpec as P

MESH = pl.DeviceIdType.MESH
F32 = jnp.float32
BF16 = jnp.bfloat16
CHUNKS = 4
COLS = 1024
WIDE = COLS // CHUNKS
LEVS = 16
ROWS = 16
HID = 1024
TILES = COLS // 128


def nt(a, b):
    return lax.dot_general(a, b, (((1,), (1,)), ((), ())), preferred_element_type=F32)


def nn(a, b):
    return jnp.dot(a, b, preferred_element_type=F32)


def sides_of(block):
    lane = lax.broadcasted_iota(jnp.int32, block.shape, 1)
    left = jnp.where(lane == 0, 0.0, pltpu.roll(block, 1, 1))
    right = jnp.where(lane == block.shape[1] - 1, 0.0, pltpu.roll(block, block.shape[1] - 1, 1))
    return left + right


def kernel(
    state_hbm, cot_hbm, diff_hbm, vinv_hbm, w_in_hbm, w_out_hbm, out_hbm,
    state_v, cot_v, diff_v, vinv_v, w_in_v, w_out_v, out_v,
    cot_f, grid_s, grid_w, adj_v,
    s_cot, r_cot, s_state, r_state, s_adj, r_adj,
    w_in_p, w_in_t, w_out_t, v_fwd, v_adj, gain,
    in_sems, tile_sems, cot_sems, state_sems, adj_sems, halo_a, halo_b,
):
    me = lax.axis_index("lev")
    hor = lax.axis_index("hor")
    last = lax.axis_size("hor") - 1

    def tiles(wide, tall, sem, out=False):
        pairs = [(wide.at[:, pl.ds(t * 128, 128)], tall.at[t]) for t in range(TILES)]
        return [pltpu.make_async_copy(b, a, sem.at[t]) if out else pltpu.make_async_copy(a, b, sem.at[t])
                for t, (a, b) in enumerate(pairs)]

    cot_load = pltpu.make_async_copy(cot_hbm, cot_v, in_sems.at[0])
    state_load = tiles(state_hbm, state_v, tile_sems.at[0])
    rest = tiles(diff_hbm, diff_v, tile_sems.at[1]) + [
        pltpu.make_async_copy(src, dst, in_sems.at[i + 1])
        for i, (src, dst) in enumerate(((vinv_hbm, vinv_v), (w_in_hbm, w_in_v), (w_out_hbm, w_out_v)))
    ]
    loads = [cot_load] + state_load + rest
    for load in loads:
        load.start()

    barrier = pltpu.get_barrier_semaphore()

    @pl.loop(1, LEVS)
    def _(j):
        pl.semaphore_signal(
            barrier, inc=1, device_id={"lev": lax.rem(me + j, LEVS), "hor": hor}, device_id_type=MESH
        )

    @pl.when(hor > 0)
    def _():
        pl.semaphore_signal(barrier, inc=1, device_id={"lev": me, "hor": hor - 1}, device_id_type=MESH)

    @pl.when(hor < last)
    def _():
        pl.semaphore_signal(barrier, inc=1, device_id={"lev": me, "hor": hor + 1}, device_id_type=MESH)

    def slot(r):
        depth = jnp.minimum(r, ROWS - 1 - r)
        return depth // 2, lax.rem(depth, 2) * 8 + (r >= ROWS // 2).astype(jnp.int32) * 4

    def put(buf, r, row):
        c, first = slot(r)
        for i in range(4):
            buf[c, first + i] = row[:, i * WIDE:(i + 1) * WIDE]

    def take(buf, r):
        c, first = slot(r)
        return jnp.concatenate([buf[c, first + i] for i in range(4)], axis=1).astype(F32)

    def across(ref, base, lo=0, hi=COLS):
        return jnp.concatenate(
            [ref[t, pl.ds(base, 8, stride=ROWS), :] for t in range(lo // 128, hi // 128)], axis=1
        )

    def both(ref, r):
        return jnp.concatenate([across(ref, r), across(ref, 128 + r)], axis=0)

    def doubled(ref, r, lo=0, hi=COLS):
        coef = across(ref, r, lo, hi)
        return jnp.concatenate([coef, coef], axis=0)

    cot_load.wait()
    for t in range(TILES):
        cot_f[t] = cot_v[:, t * 128:(t + 1) * 128].astype(F32)

    @pl.loop(0, ROWS)
    def _(r):
        put(s_cot, r, both(cot_f, r).astype(BF16))

    for c in range(CHUNKS):
        r_cot[c, me] = s_cot[c, me]

    for load in state_load:
        load.wait()

    @pl.loop(0, ROWS)
    def _(r):
        grid_s[r + 1] = both(state_v, r)

    @pl.when(hor == 0)
    def _():
        grid_s[0] = jnp.zeros((16, COLS), F32)
        grid_w[0] = jnp.zeros((16, COLS), F32)

    @pl.when(hor == last)
    def _():
        grid_s[ROWS + 1] = jnp.zeros((16, COLS), F32)
        grid_w[ROWS + 1] = jnp.zeros((16, COLS), F32)

    for load in rest:
        load.wait()

    pl.semaphore_wait(
        barrier, LEVS - 1 + (hor > 0).astype(jnp.int32) + (hor < last).astype(jnp.int32)
    )

    def edge(grid, sems, up, cols):
        src, dst = (ROWS, 0) if up else (1, ROWS + 1)
        return pltpu.make_async_remote_copy(
            src_ref=grid.at[src, :, cols], dst_ref=grid.at[dst, :, cols],
            send_sem=sems.at[0, int(up)], recv_sem=sems.at[1, int(up)],
            device_id={"lev": me, "hor": hor + (1 if up else -1)}, device_id_type=MESH,
        )

    def swap_start(grid, sems, cols):
        @pl.when(hor > 0)
        def _():
            edge(grid, sems, False, cols).start()

        @pl.when(hor < last)
        def _():
            edge(grid, sems, True, cols).start()

    def swap_wait(grid, sems, cols):
        @pl.when(hor > 0)
        def _():
            edge(grid, sems, False, cols).wait_send()
            edge(grid, sems, True, cols).wait_recv()

        @pl.when(hor < last)
        def _():
            edge(grid, sems, True, cols).wait_send()
            edge(grid, sems, False, cols).wait_recv()

    def spread(src, dst, sems, c):
        @pl.loop(1, LEVS)
        def _(j):
            peer = lax.rem(me + j, LEVS)
            pltpu.make_async_remote_copy(
                src_ref=src.at[c, peer], dst_ref=dst.at[c, me],
                send_sem=sems.at[0, c], recv_sem=sems.at[1, c],
                device_id={"lev": peer, "hor": hor}, device_id_type=MESH,
            ).start()

    def gathered(buf, sems, way, c):
        part = buf.at[c, pl.ds(0, LEVS - 1)]
        pltpu.make_async_copy(part, part, sems.at[way, c]).wait()

    full = pl.ds(0, COLS)
    swap_start(grid_s, halo_a, full)
    for c in range(CHUNKS):
        spread(s_cot, r_cot, cot_sems, c)

    swap_wait(grid_s, halo_a, full)

    @pl.loop(0, ROWS)
    def _(r):
        mid = grid_s[r + 1]
        around = grid_s[r] + grid_s[r + 2] + sides_of(mid) - 4.0 * mid
        put(s_state, r, (mid + doubled(diff_v, r) * around).astype(BF16))

    for c in range(CHUNKS):
        spread(s_state, r_state, state_sems, c)
    for c in range(CHUNKS):
        r_state[c, me] = s_state[c, me]

    at_p = lax.broadcasted_iota(jnp.int32, (256, 256), 0)
    at_k = lax.broadcasted_iota(jnp.int32, (256, 256), 1)
    place = (at_p // 16) * 8 + (at_p % 16) // 8 * 128 + at_p % 8
    perm_t = (place == at_k).astype(F32).astype(BF16)
    w_in_p[...] = nt(w_in_v[...], perm_t).astype(BF16)
    w_in_t[...] = nt(perm_t, w_in_v[...]).astype(BF16)
    w_out_t[...] = nn(perm_t, w_out_v[...]).T.astype(BF16)
    eye = lax.broadcasted_iota(jnp.int32, (128, 128), 0) == lax.broadcasted_iota(jnp.int32, (128, 128), 1)
    parts = [jnp.zeros((256, 256), F32) for _ in range(2)]
    for f in range(2):
        exact = vinv_v[f]
        high = exact.astype(BF16)
        low = (exact - high.astype(F32)).astype(BF16)
        sel = perm_t[:, f * 128:(f + 1) * 128]
        for i, piece in enumerate((high, low)):
            parts[i] += nn(sel, nt(piece, sel).astype(BF16))
        diag = jnp.sum(jnp.where(eye, exact, 0.0), axis=1, keepdims=True)
        for src in range(LEVS):
            gain[src * 16 + f * 8:src * 16 + f * 8 + 8, :] = jnp.broadcast_to(
                diag[src * 8:src * 8 + 8], (8, 128)
            )
    for i in range(2):
        v_fwd[:, i * 256:(i + 1) * 256] = parts[i].astype(BF16)
    high_t = parts[0].T.astype(BF16)
    v_adj[:, 0:256] = high_t
    v_adj[:, 256:512] = high_t
    v_adj[:, 512:768] = parts[1].T.astype(BF16)

    def columns(c):
        diffused = r_state[c].reshape(256, WIDE)
        cot = r_cot[c].reshape(256, WIDE)
        solved = nn(v_fwd[...], jnp.concatenate([diffused, diffused], axis=0))
        inputs = solved.astype(BF16)
        level = cot.astype(F32)
        for h in range(4):
            hs = slice(h * 256, (h + 1) * 256)
            preact = nn(w_in_p[hs, :], inputs)
            hidden = nn(w_out_t[hs, :], cot)
            s = 0.5 + 0.5 * jnp.tanh(0.5 * preact)
            pre = (hidden * s * (1.0 + preact * (1.0 - s))).astype(BF16)
            level = level + nn(w_in_t[:, hs], pre)
        high = level.astype(BF16)
        low = (level - high.astype(F32)).astype(BF16)
        adjoint = nn(v_adj[...], jnp.concatenate([high, low, high], axis=0))
        delta = adjoint - gain[:, 0:1] * cot.astype(F32)
        s_adj[c] = delta.astype(BF16).reshape(LEVS, 16, WIDE)

    @pl.loop(0, CHUNKS)
    def _(c):
        gathered(r_cot, cot_sems, 1, c)
        gathered(r_state, state_sems, 1, c)
        columns(c)
        spread(s_adj, r_adj, adj_sems, c)
        r_adj[c, me] = s_adj[c, me]

    scale = gain[pl.ds(pl.multiple_of(me * 16, 16), 16), 0:1]

    def stencil(r):
        mid = grid_w[r + 1]
        row = adj_v[r] + (grid_w[r] + grid_w[r + 2] + sides_of(mid) - 4.0 * mid)
        for t in range(TILES):
            out_v[t, pl.ds(r, 8, stride=ROWS), :] = row[0:8, t * 128:(t + 1) * 128]
            out_v[t, pl.ds(128 + r, 8, stride=ROWS), :] = row[8:16, t * 128:(t + 1) * 128]

    def mirrored(start, stop, one):
        @pl.loop(start, stop)
        def _(r):
            one(r)
            one(ROWS - 1 - r)

    def weigh(r):
        adj = take(r_adj, r) + scale * take(s_cot, r)
        adj_v[r] = adj
        grid_w[r + 1] = doubled(diff_v, r) * adj

    for c in range(CHUNKS):
        gathered(r_adj, adj_sems, 1, c)
        mirrored(2 * c, 2 * c + 2, weigh)
        if c == 0:
            swap_start(grid_w, halo_b, full)
        if c == CHUNKS - 2:
            swap_wait(grid_w, halo_b, full)
            mirrored(0, 1, stencil)
        mirrored(max(1, 2 * c - 1), 2 * c + (2 if c == CHUNKS - 1 else 1), stencil)

    stores = tiles(out_hbm, out_v, tile_sems.at[2], out=True)
    for store in stores:
        store.start()
    for c in range(CHUNKS):
        gathered(s_cot, cot_sems, 0, c)
        gathered(s_state, state_sems, 0, c)
        gathered(s_adj, adj_sems, 0, c)
    for store in stores:
        store.wait()


def body(state, cotangent, diffusion, vertical_inverse, w_in, w_out):
    dma = pltpu.SemaphoreType.DMA
    slabs = (CHUNKS, LEVS, 16, WIDE)
    out = pl.pallas_call(
        kernel,
        out_shape=pltpu.VMEM((256, COLS), F32),
        in_specs=[pl.BlockSpec(memory_space=pltpu.HBM)] * 6,
        out_specs=pl.BlockSpec(memory_space=pltpu.VMEM),
        scratch_shapes=[
            pltpu.VMEM((TILES, 256, 128), F32), pltpu.VMEM((256, COLS), BF16), pltpu.VMEM((TILES, 128, 128), F32),
            pltpu.VMEM((2, 128, 128), F32), pltpu.VMEM((HID, 256), BF16), pltpu.VMEM((256, HID), BF16),
            pltpu.VMEM((TILES, 256, 128), F32),
            pltpu.VMEM((TILES, 256, 128), F32), pltpu.VMEM((ROWS + 2, 16, COLS), F32),
            pltpu.VMEM((ROWS + 2, 16, COLS), F32), pltpu.VMEM((ROWS, 16, COLS), F32),
        ] + [pltpu.VMEM(slabs, BF16)] * 6 + [
            pltpu.VMEM((HID, 256), BF16), pltpu.VMEM((256, HID), BF16), pltpu.VMEM((HID, 256), BF16),
            pltpu.VMEM((256, 512), BF16), pltpu.VMEM((256, 768), BF16), pltpu.VMEM((256, 128), F32),
            dma((4,)), dma((3, TILES)), dma((2, CHUNKS)), dma((2, CHUNKS)), dma((2, CHUNKS)), dma((2, 2)), dma((2, 2)),
        ],
        compiler_params=pltpu.CompilerParams(
            collective_id=0, has_side_effects=True, vmem_limit_bytes=44 << 20
        ),
    )(*[
        pltpu.with_memory_space_constraint(x, pltpu.HBM)
        for x in (state.reshape(256, COLS), cotangent.reshape(256, COLS), diffusion.reshape(128, COLS),
                  vertical_inverse, w_in, w_out)
    ])
    return out.reshape(2, 8, ROWS, COLS)


def solution(mesh):
    placed = (
        P(None, "lev", "hor", None),
        P(None, "lev", "hor", None),
        P("lev", "hor", None),
        P(),
        P(),
        P(),
    )
    return jax.shard_map(
        body, mesh=mesh, in_specs=placed, out_specs=P(None, "lev", "hor", None), check_vma=False
    )
```

```python
import functools

import jax
import jax.numpy as jnp
from jax import lax
from jax.experimental import pallas as pl
from jax.experimental.pallas import tpu as pltpu
from jax.sharding import PartitionSpec as P

MESH = pl.DeviceIdType.MESH
F32 = jnp.float32
BF16 = jnp.bfloat16
CHUNKS = 4
COLS = 1024
WIDE = COLS // CHUNKS
LEVS = 16
ROWS = 16
HID = 1024
AHEAD = 4
TILES = COLS // 128


def nt(a, b):
    return lax.dot_general(a, b, (((1,), (1,)), ((), ())), preferred_element_type=F32)


def nn(a, b):
    return jnp.dot(a, b, preferred_element_type=F32)


def sides_of(block):
    lane = lax.broadcasted_iota(jnp.int32, block.shape, 1)
    left = jnp.where(lane == 0, 0.0, pltpu.roll(block, 1, 1))
    right = jnp.where(lane == block.shape[1] - 1, 0.0, pltpu.roll(block, block.shape[1] - 1, 1))
    return left + right


def kernel(
    state_hbm, cot_hbm, diff_hbm, vinv_hbm, w_in_hbm, w_out_hbm, out_hbm,
    state_v, cot_v, diff_v, vinv_v, w_in_v, w_out_v, out_v,
    cot_f, grid_s, grid_w, adj_v,
    s_edge, r_edge, s_cot, r_cot, s_state, r_state, s_adj, r_adj,
    w_in_p, w_in_t, w_out_t, v_fwd, v_adj, gain,
    in_sems, tile_sems, cot_sems, state_sems, adj_sems, edge_sems, pace,
):
    me = lax.axis_index("lev")
    hor = lax.axis_index("hor")
    last = lax.axis_size("hor") - 1

    def tiles(wide, tall, sem, out=False):
        pairs = [(wide.at[:, pl.ds(t * 128, 128)], tall.at[t]) for t in range(TILES)]
        return [pltpu.make_async_copy(b, a, sem.at[t]) if out else pltpu.make_async_copy(a, b, sem.at[t])
                for t, (a, b) in enumerate(pairs)]

    cot_load = pltpu.make_async_copy(cot_hbm, cot_v, in_sems.at[0])
    state_load = tiles(state_hbm, state_v, tile_sems.at[0])
    rest = tiles(diff_hbm, diff_v, tile_sems.at[1]) + [
        pltpu.make_async_copy(src, dst, in_sems.at[i + 1])
        for i, (src, dst) in enumerate(((vinv_hbm, vinv_v), (w_in_hbm, w_in_v), (w_out_hbm, w_out_v)))
    ]
    loads = [cot_load] + state_load + rest
    for load in loads:
        load.start()

    barrier = pltpu.get_barrier_semaphore()

    @pl.loop(1, LEVS)
    def _(j):
        pl.semaphore_signal(
            barrier, inc=1, device_id={"lev": lax.rem(me + j, LEVS), "hor": hor}, device_id_type=MESH
        )

    @pl.when(hor > 0)
    def _():
        pl.semaphore_signal(barrier, inc=1, device_id={"lev": me, "hor": hor - 1}, device_id_type=MESH)

    @pl.when(hor < last)
    def _():
        pl.semaphore_signal(barrier, inc=1, device_id={"lev": me, "hor": hor + 1}, device_id_type=MESH)

    flipped = me + 2 - 4 * (lax.rem(me, 4) // 2)
    stack = []
    for step in (4, -4):
        wraps = hor + step > last if step > 0 else hor + step < 0
        stack.append({
            "lev": jnp.where(wraps, flipped, me),
            "hor": lax.rem(hor + step + last + 1, last + 1),
        })
    for neighbour in stack:
        pl.semaphore_signal(barrier, inc=1, device_id=neighbour, device_id_type=MESH)

    def slot(r):
        depth = jnp.minimum(r, ROWS - 1 - r)
        return depth // 2, lax.rem(depth, 2) * 8 + (r >= ROWS // 2).astype(jnp.int32) * 4

    def put(buf, r, row):
        c, first = slot(r)
        for i in range(4):
            buf[c, first + i] = row[:, i * WIDE:(i + 1) * WIDE]

    def take(buf, r):
        c, first = slot(r)
        return jnp.concatenate([buf[c, first + i] for i in range(4)], axis=1).astype(F32)

    def across(ref, base, lo=0, hi=COLS):
        return jnp.concatenate(
            [ref[t, pl.ds(base, 8, stride=ROWS), :] for t in range(lo // 128, hi // 128)], axis=1
        )

    def both(ref, r):
        return jnp.concatenate([across(ref, r), across(ref, 128 + r)], axis=0)

    def doubled(ref, r, lo=0, hi=COLS):
        coef = across(ref, r, lo, hi)
        return jnp.concatenate([coef, coef], axis=0)

    cot_load.wait()
    for t in range(TILES):
        cot_f[t] = cot_v[:, t * 128:(t + 1) * 128].astype(F32)

    @pl.loop(0, ROWS)
    def _(r):
        put(s_cot, r, both(cot_f, r).astype(BF16))

    for c in range(CHUNKS):
        r_cot[c, me] = s_cot[c, me]

    for load in state_load:
        load.wait()

    for r in (0, ROWS - 1):
        grid_s[r + 1] = both(state_v, r)

    @pl.when(hor == 0)
    def _():
        grid_s[0] = jnp.zeros((16, COLS), F32)
        grid_w[0] = jnp.zeros((16, COLS), F32)

    @pl.when(hor == last)
    def _():
        grid_s[ROWS + 1] = jnp.zeros((16, COLS), F32)
        grid_w[ROWS + 1] = jnp.zeros((16, COLS), F32)

    pl.semaphore_wait(
        barrier, LEVS + 1 + (hor > 0).astype(jnp.int32) + (hor < last).astype(jnp.int32)
    )

    def edge(k, up):
        return pltpu.make_async_remote_copy(
            src_ref=s_edge.at[k, up], dst_ref=r_edge.at[k, up],
            send_sem=edge_sems.at[0, k, up], recv_sem=edge_sems.at[1, k, up],
            device_id={"lev": me, "hor": hor + 2 * up - 1}, device_id_type=MESH,
        )

    def swap_start(k, grid):
        @pl.when(hor > 0)
        def _():
            s_edge[k, 0] = grid[1].astype(BF16)
            edge(k, 0).start()

        @pl.when(hor < last)
        def _():
            s_edge[k, 1] = grid[ROWS].astype(BF16)
            edge(k, 1).start()

    def swap_wait(k, grid):
        @pl.when(hor > 0)
        def _():
            edge(k, 0).wait_send()
            edge(k, 1).wait_recv()
            grid[0] = r_edge[k, 1].astype(F32)

        @pl.when(hor < last)
        def _():
            edge(k, 1).wait_send()
            edge(k, 0).wait_recv()
            grid[ROWS + 1] = r_edge[k, 0].astype(F32)

    def spread(src, dst, sems, c):
        @pl.loop(1, LEVS)
        def _(j):
            peer = lax.rem(me + j, LEVS)
            pltpu.make_async_remote_copy(
                src_ref=src.at[c, peer], dst_ref=dst.at[c, me],
                send_sem=sems.at[0, c], recv_sem=sems.at[1, c],
                device_id={"lev": peer, "hor": hor}, device_id_type=MESH,
            ).start()

    def gathered(buf, sems, way, c):
        part = buf.at[c, pl.ds(0, LEVS - 1)]
        pltpu.make_async_copy(part, part, sems.at[way, c]).wait()

    swap_start(0, grid_s)
    for c in range(CHUNKS):
        spread(s_cot, r_cot, cot_sems, c)

    for load in rest:
        load.wait()

    @pl.loop(1, ROWS - 1)
    def _(r):
        grid_s[r + 1] = both(state_v, r)

    swap_wait(0, grid_s)

    @pl.loop(0, ROWS)
    def _(r):
        mid = grid_s[r + 1]
        around = grid_s[r] + grid_s[r + 2] + sides_of(mid) - 4.0 * mid
        put(s_state, r, (mid + doubled(diff_v, r) * around).astype(BF16))

    at_p = lax.broadcasted_iota(jnp.int32, (256, 256), 0)
    at_k = lax.broadcasted_iota(jnp.int32, (256, 256), 1)
    place = (at_p // 16) * 8 + (at_p % 16) // 8 * 128 + at_p % 8
    perm_t = (place == at_k).astype(F32).astype(BF16)
    w_in_p[...] = nt(w_in_v[...], perm_t).astype(BF16)
    w_in_t[...] = nt(perm_t, w_in_v[...]).astype(BF16)
    w_out_t[...] = nn(perm_t, w_out_v[...]).T.astype(BF16)
    eye = lax.broadcasted_iota(jnp.int32, (128, 128), 0) == lax.broadcasted_iota(jnp.int32, (128, 128), 1)
    parts = [jnp.zeros((256, 256), F32) for _ in range(2)]
    for f in range(2):
        exact = vinv_v[f]
        high = exact.astype(BF16)
        low = (exact - high.astype(F32)).astype(BF16)
        sel = perm_t[:, f * 128:(f + 1) * 128]
        for i, piece in enumerate((high, low)):
            parts[i] += nn(sel, nt(piece, sel).astype(BF16))
        diag = jnp.sum(jnp.where(eye, exact, 0.0), axis=1, keepdims=True)
        for src in range(LEVS):
            gain[src * 16 + f * 8:src * 16 + f * 8 + 8, :] = jnp.broadcast_to(
                diag[src * 8:src * 8 + 8], (8, 128)
            )
    for i in range(2):
        v_fwd[:, i * 256:(i + 1) * 256] = parts[i].astype(BF16)
    high_t = parts[0].T.astype(BF16)
    v_adj[:, 0:256] = high_t
    v_adj[:, 256:512] = high_t
    v_adj[:, 512:768] = parts[1].T.astype(BF16)

    steps = [(s_cot, r_cot, cot_sems, c) for c in range(CHUNKS)]
    steps += [(s_state, r_state, state_sems, c) for c in range(CHUNKS)]
    for k in range(CHUNKS, len(steps)):
        if k >= AHEAD:
            before = steps[k - AHEAD]
            gathered(before[1], before[2], 1, before[3])
            for i, neighbour in enumerate(stack):
                pl.semaphore_signal(pace.at[i], inc=1, device_id=neighbour, device_id_type=MESH)
            for i in range(2):
                pl.semaphore_wait(pace.at[i], 1)
        spread(*steps[k])
    done = len(steps) - AHEAD

    for c in range(CHUNKS):
        r_state[c, me] = s_state[c, me]

    def columns(c):
        diffused = r_state[c].reshape(256, WIDE)
        cot = r_cot[c].reshape(256, WIDE)
        solved = nn(v_fwd[...], jnp.concatenate([diffused, diffused], axis=0))
        inputs = solved.astype(BF16)
        level = cot.astype(F32)
        for h in range(4):
            hs = slice(h * 256, (h + 1) * 256)
            preact = nn(w_in_p[hs, :], inputs)
            hidden = nn(w_out_t[hs, :], cot)
            s = 0.5 + 0.5 * jnp.tanh(0.5 * preact)
            pre = (hidden * s * (1.0 + preact * (1.0 - s))).astype(BF16)
            level = level + nn(w_in_t[:, hs], pre)
        high = level.astype(BF16)
        low = (level - high.astype(F32)).astype(BF16)
        adjoint = nn(v_adj[...], jnp.concatenate([high, low, high], axis=0))
        delta = adjoint - gain[:, 0:1] * cot.astype(F32)
        s_adj[c] = delta.astype(BF16).reshape(LEVS, 16, WIDE)

    @pl.loop(0, CHUNKS)
    def _(c):
        @pl.when(c >= done)
        def _():
            gathered(r_cot, cot_sems, 1, c)

        gathered(r_state, state_sems, 1, c)
        columns(c)
        spread(s_adj, r_adj, adj_sems, c)
        r_adj[c, me] = s_adj[c, me]

    scale = gain[pl.ds(pl.multiple_of(me * 16, 16), 16), 0:1]

    def stencil(r):
        mid = grid_w[r + 1]
        row = adj_v[r] + (grid_w[r] + grid_w[r + 2] + sides_of(mid) - 4.0 * mid)
        for t in range(TILES):
            out_v[t, pl.ds(r, 8, stride=ROWS), :] = row[0:8, t * 128:(t + 1) * 128]
            out_v[t, pl.ds(128 + r, 8, stride=ROWS), :] = row[8:16, t * 128:(t + 1) * 128]

    def mirrored(start, stop, one):
        @pl.loop(start, stop)
        def _(r):
            one(r)
            one(ROWS - 1 - r)

    def weigh(r):
        adj = take(r_adj, r) + scale * take(s_cot, r)
        adj_v[r] = adj
        grid_w[r + 1] = doubled(diff_v, r) * adj

    for c in range(CHUNKS):
        gathered(r_adj, adj_sems, 1, c)
        mirrored(2 * c, 2 * c + 2, weigh)
        if c == 0:
            swap_start(1, grid_w)
        if c == CHUNKS - 2:
            swap_wait(1, grid_w)
            mirrored(0, 1, stencil)
        mirrored(max(1, 2 * c - 1), 2 * c + (2 if c == CHUNKS - 1 else 1), stencil)

    stores = tiles(out_hbm, out_v, tile_sems.at[2], out=True)
    for store in stores:
        store.start()
    for c in range(CHUNKS):
        gathered(s_cot, cot_sems, 0, c)
        gathered(s_state, state_sems, 0, c)
        gathered(s_adj, adj_sems, 0, c)
    for store in stores:
        store.wait()


def body(state, cotangent, diffusion, vertical_inverse, w_in, w_out):
    dma = pltpu.SemaphoreType.DMA
    slabs = (CHUNKS, LEVS, 16, WIDE)
    out = pl.pallas_call(
        kernel,
        out_shape=pltpu.VMEM((256, COLS), F32),
        in_specs=[pl.BlockSpec(memory_space=pltpu.HBM)] * 6,
        out_specs=pl.BlockSpec(memory_space=pltpu.VMEM),
        scratch_shapes=[
            pltpu.VMEM((TILES, 256, 128), F32), pltpu.VMEM((256, COLS), BF16), pltpu.VMEM((TILES, 128, 128), F32),
            pltpu.VMEM((2, 128, 128), F32), pltpu.VMEM((HID, 256), BF16), pltpu.VMEM((256, HID), BF16),
            pltpu.VMEM((TILES, 256, 128), F32),
            pltpu.VMEM((TILES, 256, 128), F32), pltpu.VMEM((ROWS + 2, 16, COLS), F32),
            pltpu.VMEM((ROWS + 2, 16, COLS), F32), pltpu.VMEM((ROWS, 16, COLS), F32),
        ] + [pltpu.VMEM((2, 2, 16, COLS), BF16)] * 2 + [pltpu.VMEM(slabs, BF16)] * 6 + [
            pltpu.VMEM((HID, 256), BF16), pltpu.VMEM((256, HID), BF16), pltpu.VMEM((HID, 256), BF16),
            pltpu.VMEM((256, 512), BF16), pltpu.VMEM((256, 768), BF16), pltpu.VMEM((256, 128), F32),
            dma((4,)), dma((3, TILES)), dma((2, CHUNKS)), dma((2, CHUNKS)), dma((2, CHUNKS)), dma((2, 2, 2)), pltpu.SemaphoreType.REGULAR((2,)),
        ],
        compiler_params=pltpu.CompilerParams(
            collective_id=0, has_side_effects=True, vmem_limit_bytes=44 << 20
        ),
    )(*[
        pltpu.with_memory_space_constraint(x, pltpu.HBM)
        for x in (state.reshape(256, COLS), cotangent.reshape(256, COLS), diffusion.reshape(128, COLS),
                  vertical_inverse, w_in, w_out)
    ])
    return out.reshape(2, 8, ROWS, COLS)


def solution(mesh):
    placed = (
        P(None, "lev", "hor", None),
        P(None, "lev", "hor", None),
        P("lev", "hor", None),
        P(),
        P(),
        P(),
    )
    return jax.shard_map(
        body, mesh=mesh, in_specs=placed, out_specs=P(None, "lev", "hor", None), check_vma=False
    )
```

```python
import functools

import jax
import jax.numpy as jnp
from jax import lax
from jax.experimental import pallas as pl
from jax.experimental.pallas import tpu as pltpu
from jax.sharding import PartitionSpec as P

MESH = pl.DeviceIdType.MESH
F32 = jnp.float32
BF16 = jnp.bfloat16
CHUNKS = 4
COLS = 1024
WIDE = COLS // CHUNKS
LEVS = 16
ROWS = 16
HID = 1024
AHEAD = 4
TILES = COLS // 128


def nt(a, b):
    return lax.dot_general(a, b, (((1,), (1,)), ((), ())), preferred_element_type=F32)


def nn(a, b):
    return jnp.dot(a, b, preferred_element_type=F32)


def sides_of(block):
    lane = lax.broadcasted_iota(jnp.int32, block.shape, 1)
    left = jnp.where(lane == 0, 0.0, pltpu.roll(block, 1, 1))
    right = jnp.where(lane == block.shape[1] - 1, 0.0, pltpu.roll(block, block.shape[1] - 1, 1))
    return left + right


def kernel(
    state_hbm, cot_hbm, diff_hbm, vinv_hbm, w_in_hbm, w_out_hbm, out_hbm,
    state_v, cot_v, diff_v, vinv_v, w_in_v, w_out_v, out_v,
    cot_f, grid_s, grid_w, adj_v,
    s_edge, r_edge, s_cot, r_cot, s_state, r_state, s_adj, r_adj,
    w_in_p, w_in_t, w_out_t, v_fwd, v_adj, gain,
    in_sems, tile_sems, cot_sems, state_sems, adj_sems, edge_sems,
):
    me = lax.axis_index("lev")
    hor = lax.axis_index("hor")
    last = lax.axis_size("hor") - 1

    def tiles(wide, tall, sem, out=False):
        pairs = [(wide.at[:, pl.ds(t * 128, 128)], tall.at[t]) for t in range(TILES)]
        return [pltpu.make_async_copy(b, a, sem.at[t]) if out else pltpu.make_async_copy(a, b, sem.at[t])
                for t, (a, b) in enumerate(pairs)]

    cot_load = pltpu.make_async_copy(cot_hbm, cot_v, in_sems.at[0])
    state_load = tiles(state_hbm, state_v, tile_sems.at[0])
    rest = tiles(diff_hbm, diff_v, tile_sems.at[1]) + [
        pltpu.make_async_copy(src, dst, in_sems.at[i + 1])
        for i, (src, dst) in enumerate(((vinv_hbm, vinv_v), (w_in_hbm, w_in_v), (w_out_hbm, w_out_v)))
    ]
    loads = [cot_load] + state_load + rest
    for load in loads:
        load.start()

    barrier = pltpu.get_barrier_semaphore()

    @pl.loop(1, LEVS)
    def _(j):
        pl.semaphore_signal(
            barrier, inc=1, device_id={"lev": lax.rem(me + j, LEVS), "hor": hor}, device_id_type=MESH
        )

    @pl.when(hor > 0)
    def _():
        pl.semaphore_signal(barrier, inc=1, device_id={"lev": me, "hor": hor - 1}, device_id_type=MESH)

    @pl.when(hor < last)
    def _():
        pl.semaphore_signal(barrier, inc=1, device_id={"lev": me, "hor": hor + 1}, device_id_type=MESH)

    def slot(r):
        depth = jnp.minimum(r, ROWS - 1 - r)
        return depth // 2, lax.rem(depth, 2) * 8 + (r >= ROWS // 2).astype(jnp.int32) * 4

    def put(buf, r, row):
        c, first = slot(r)
        for i in range(4):
            buf[c, first + i] = row[:, i * WIDE:(i + 1) * WIDE]

    def take(buf, r):
        c, first = slot(r)
        return jnp.concatenate([buf[c, first + i] for i in range(4)], axis=1).astype(F32)

    def across(ref, base, lo=0, hi=COLS):
        return jnp.concatenate(
            [ref[t, pl.ds(base, 8, stride=ROWS), :] for t in range(lo // 128, hi // 128)], axis=1
        )

    def both(ref, r):
        return jnp.concatenate([across(ref, r), across(ref, 128 + r)], axis=0)

    def doubled(ref, r, lo=0, hi=COLS):
        coef = across(ref, r, lo, hi)
        return jnp.concatenate([coef, coef], axis=0)

    cot_load.wait()
    for t in range(TILES):
        cot_f[t] = cot_v[:, t * 128:(t + 1) * 128].astype(F32)

    @pl.loop(0, ROWS)
    def _(r):
        put(s_cot, r, both(cot_f, r).astype(BF16))

    for c in range(CHUNKS):
        r_cot[c, me] = s_cot[c, me]

    for load in state_load:
        load.wait()

    for r in (0, ROWS - 1):
        grid_s[r + 1] = both(state_v, r)

    @pl.when(hor == 0)
    def _():
        grid_s[0] = jnp.zeros((16, COLS), F32)
        grid_w[0] = jnp.zeros((16, COLS), F32)

    @pl.when(hor == last)
    def _():
        grid_s[ROWS + 1] = jnp.zeros((16, COLS), F32)
        grid_w[ROWS + 1] = jnp.zeros((16, COLS), F32)

    pl.semaphore_wait(
        barrier, LEVS - 1 + (hor > 0).astype(jnp.int32) + (hor < last).astype(jnp.int32)
    )

    def edge(k, up):
        return pltpu.make_async_remote_copy(
            src_ref=s_edge.at[k, up], dst_ref=r_edge.at[k, up],
            send_sem=edge_sems.at[0, k, up], recv_sem=edge_sems.at[1, k, up],
            device_id={"lev": me, "hor": hor + 2 * up - 1}, device_id_type=MESH,
        )

    def swap_start(k, grid):
        @pl.when(hor > 0)
        def _():
            s_edge[k, 0] = grid[1].astype(BF16)
            edge(k, 0).start()

        @pl.when(hor < last)
        def _():
            s_edge[k, 1] = grid[ROWS].astype(BF16)
            edge(k, 1).start()

    def swap_wait(k, grid):
        @pl.when(hor > 0)
        def _():
            edge(k, 0).wait_send()
            edge(k, 1).wait_recv()
            grid[0] = r_edge[k, 1].astype(F32)

        @pl.when(hor < last)
        def _():
            edge(k, 1).wait_send()
            edge(k, 0).wait_recv()
            grid[ROWS + 1] = r_edge[k, 0].astype(F32)

    def spread(src, dst, sems, c):
        @pl.loop(1, LEVS)
        def _(j):
            peer = lax.rem(me + j, LEVS)
            pltpu.make_async_remote_copy(
                src_ref=src.at[c, peer], dst_ref=dst.at[c, me],
                send_sem=sems.at[0, c], recv_sem=sems.at[1, c],
                device_id={"lev": peer, "hor": hor}, device_id_type=MESH,
            ).start()

    def gathered(buf, sems, way, c):
        part = buf.at[c, pl.ds(0, LEVS - 1)]
        pltpu.make_async_copy(part, part, sems.at[way, c]).wait()

    swap_start(0, grid_s)
    for c in range(CHUNKS):
        spread(s_cot, r_cot, cot_sems, c)

    for load in rest:
        load.wait()

    @pl.loop(1, ROWS - 1)
    def _(r):
        grid_s[r + 1] = both(state_v, r)

    swap_wait(0, grid_s)

    @pl.loop(0, ROWS)
    def _(r):
        mid = grid_s[r + 1]
        around = grid_s[r] + grid_s[r + 2] + sides_of(mid) - 4.0 * mid
        put(s_state, r, (mid + doubled(diff_v, r) * around).astype(BF16))

    at_p = lax.broadcasted_iota(jnp.int32, (256, 256), 0)
    at_k = lax.broadcasted_iota(jnp.int32, (256, 256), 1)
    place = (at_p // 16) * 8 + (at_p % 16) // 8 * 128 + at_p % 8
    perm_t = (place == at_k).astype(F32).astype(BF16)
    w_in_p[...] = nt(w_in_v[...], perm_t).astype(BF16)
    w_in_t[...] = nt(perm_t, w_in_v[...]).astype(BF16)
    w_out_t[...] = nn(perm_t, w_out_v[...]).T.astype(BF16)
    eye = lax.broadcasted_iota(jnp.int32, (128, 128), 0) == lax.broadcasted_iota(jnp.int32, (128, 128), 1)
    parts = [jnp.zeros((256, 256), F32) for _ in range(2)]
    for f in range(2):
        exact = vinv_v[f]
        high = exact.astype(BF16)
        low = (exact - high.astype(F32)).astype(BF16)
        sel = perm_t[:, f * 128:(f + 1) * 128]
        for i, piece in enumerate((high, low)):
            parts[i] += nn(sel, nt(piece, sel).astype(BF16))
        diag = jnp.sum(jnp.where(eye, exact, 0.0), axis=1, keepdims=True)
        for src in range(LEVS):
            gain[src * 16 + f * 8:src * 16 + f * 8 + 8, :] = jnp.broadcast_to(
                diag[src * 8:src * 8 + 8], (8, 128)
            )
    for i in range(2):
        v_fwd[:, i * 256:(i + 1) * 256] = parts[i].astype(BF16)
    high_t = parts[0].T.astype(BF16)
    v_adj[:, 0:256] = high_t
    v_adj[:, 256:512] = high_t
    v_adj[:, 512:768] = parts[1].T.astype(BF16)

    steps = [(s_cot, r_cot, cot_sems, c) for c in range(CHUNKS)]
    steps += [(s_state, r_state, state_sems, c) for c in range(CHUNKS)]
    for k in range(CHUNKS, len(steps)):
        if k >= AHEAD:
            before = steps[k - AHEAD]
            gathered(before[1], before[2], 1, before[3])
        spread(*steps[k])
    done = len(steps) - AHEAD

    for c in range(CHUNKS):
        r_state[c, me] = s_state[c, me]

    def columns(c):
        diffused = r_state[c].reshape(256, WIDE)
        cot = r_cot[c].reshape(256, WIDE)
        solved = nn(v_fwd[...], jnp.concatenate([diffused, diffused], axis=0))
        inputs = solved.astype(BF16)
        level = cot.astype(F32)
        for h in range(4):
            hs = slice(h * 256, (h + 1) * 256)
            preact = nn(w_in_p[hs, :], inputs)
            hidden = nn(w_out_t[hs, :], cot)
            s = 0.5 + 0.5 * jnp.tanh(0.5 * preact)
            pre = (hidden * s * (1.0 + preact * (1.0 - s))).astype(BF16)
            level = level + nn(w_in_t[:, hs], pre)
        high = level.astype(BF16)
        low = (level - high.astype(F32)).astype(BF16)
        adjoint = nn(v_adj[...], jnp.concatenate([high, low, high], axis=0))
        delta = adjoint - gain[:, 0:1] * cot.astype(F32)
        s_adj[c] = delta.astype(BF16).reshape(LEVS, 16, WIDE)

    @pl.loop(0, CHUNKS)
    def _(c):
        @pl.when(c >= done)
        def _():
            gathered(r_cot, cot_sems, 1, c)

        gathered(r_state, state_sems, 1, c)
        columns(c)
        spread(s_adj, r_adj, adj_sems, c)
        r_adj[c, me] = s_adj[c, me]

    scale = gain[pl.ds(pl.multiple_of(me * 16, 16), 16), 0:1]

    def stencil(r):
        mid = grid_w[r + 1]
        row = adj_v[r] + (grid_w[r] + grid_w[r + 2] + sides_of(mid) - 4.0 * mid)
        for t in range(TILES):
            out_v[t, pl.ds(r, 8, stride=ROWS), :] = row[0:8, t * 128:(t + 1) * 128]
            out_v[t, pl.ds(128 + r, 8, stride=ROWS), :] = row[8:16, t * 128:(t + 1) * 128]

    def mirrored(start, stop, one):
        @pl.loop(start, stop)
        def _(r):
            one(r)
            one(ROWS - 1 - r)

    def weigh(r):
        adj = take(r_adj, r) + scale * take(s_cot, r)
        adj_v[r] = adj
        grid_w[r + 1] = doubled(diff_v, r) * adj

    for c in range(CHUNKS):
        gathered(r_adj, adj_sems, 1, c)
        mirrored(2 * c, 2 * c + 2, weigh)
        if c == 0:
            swap_start(1, grid_w)
        if c == CHUNKS - 2:
            swap_wait(1, grid_w)
            mirrored(0, 1, stencil)
        mirrored(max(1, 2 * c - 1), 2 * c + (2 if c == CHUNKS - 1 else 1), stencil)

    stores = tiles(out_hbm, out_v, tile_sems.at[2], out=True)
    for store in stores:
        store.start()
    for c in range(CHUNKS):
        gathered(s_cot, cot_sems, 0, c)
        gathered(s_state, state_sems, 0, c)
        gathered(s_adj, adj_sems, 0, c)
    for store in stores:
        store.wait()


def body(state, cotangent, diffusion, vertical_inverse, w_in, w_out):
    dma = pltpu.SemaphoreType.DMA
    slabs = (CHUNKS, LEVS, 16, WIDE)
    out = pl.pallas_call(
        kernel,
        out_shape=pltpu.VMEM((256, COLS), F32),
        in_specs=[pl.BlockSpec(memory_space=pltpu.HBM)] * 6,
        out_specs=pl.BlockSpec(memory_space=pltpu.VMEM),
        scratch_shapes=[
            pltpu.VMEM((TILES, 256, 128), F32), pltpu.VMEM((256, COLS), BF16), pltpu.VMEM((TILES, 128, 128), F32),
            pltpu.VMEM((2, 128, 128), F32), pltpu.VMEM((HID, 256), BF16), pltpu.VMEM((256, HID), BF16),
            pltpu.VMEM((TILES, 256, 128), F32),
            pltpu.VMEM((TILES, 256, 128), F32), pltpu.VMEM((ROWS + 2, 16, COLS), F32),
            pltpu.VMEM((ROWS + 2, 16, COLS), F32), pltpu.VMEM((ROWS, 16, COLS), F32),
        ] + [pltpu.VMEM((2, 2, 16, COLS), BF16)] * 2 + [pltpu.VMEM(slabs, BF16)] * 6 + [
            pltpu.VMEM((HID, 256), BF16), pltpu.VMEM((256, HID), BF16), pltpu.VMEM((HID, 256), BF16),
            pltpu.VMEM((256, 512), BF16), pltpu.VMEM((256, 768), BF16), pltpu.VMEM((256, 128), F32),
            dma((4,)), dma((3, TILES)), dma((2, CHUNKS)), dma((2, CHUNKS)), dma((2, CHUNKS)), dma((2, 2, 2)),
        ],
        compiler_params=pltpu.CompilerParams(
            collective_id=0, has_side_effects=True, vmem_limit_bytes=44 << 20
        ),
    )(*[
        pltpu.with_memory_space_constraint(x, pltpu.HBM)
        for x in (state.reshape(256, COLS), cotangent.reshape(256, COLS), diffusion.reshape(128, COLS),
                  vertical_inverse, w_in, w_out)
    ])
    return out.reshape(2, 8, ROWS, COLS)


def solution(mesh):
    placed = (
        P(None, "lev", "hor", None),
        P(None, "lev", "hor", None),
        P("lev", "hor", None),
        P(),
        P(),
        P(),
    )
    return jax.shard_map(
        body, mesh=mesh, in_specs=placed, out_specs=P(None, "lev", "hor", None), check_vma=False
    )
```

```python
import functools

import jax
import jax.numpy as jnp
from jax import lax
from jax.experimental import pallas as pl
from jax.experimental.pallas import tpu as pltpu
from jax.sharding import PartitionSpec as P

MESH = pl.DeviceIdType.MESH
F32 = jnp.float32
BF16 = jnp.bfloat16
CHUNKS = 4
COLS = 1024
WIDE = COLS // CHUNKS
LEVS = 16
ROWS = 16
HID = 1024
AHEAD = 3
TILES = COLS // 128


def nt(a, b):
    return lax.dot_general(a, b, (((1,), (1,)), ((), ())), preferred_element_type=F32)


def nn(a, b):
    return jnp.dot(a, b, preferred_element_type=F32)


def sides_of(block):
    lane = lax.broadcasted_iota(jnp.int32, block.shape, 1)
    left = jnp.where(lane == 0, 0.0, pltpu.roll(block, 1, 1))
    right = jnp.where(lane == block.shape[1] - 1, 0.0, pltpu.roll(block, block.shape[1] - 1, 1))
    return left + right


def kernel(
    state_hbm, cot_hbm, diff_hbm, vinv_hbm, w_in_hbm, w_out_hbm, out_hbm,
    state_v, cot_v, diff_v, vinv_v, w_in_v, w_out_v, out_v,
    cot_f, grid_s, grid_w, adj_v,
    s_edge, r_edge, s_cot, r_cot, s_state, r_state, s_adj, r_adj,
    w_in_p, w_in_t, w_out_t, v_fwd, v_adj, gain,
    in_sems, tile_sems, cot_sems, state_sems, adj_sems, edge_sems,
):
    me = lax.axis_index("lev")
    hor = lax.axis_index("hor")
    last = lax.axis_size("hor") - 1

    def tiles(wide, tall, sem, out=False):
        pairs = [(wide.at[:, pl.ds(t * 128, 128)], tall.at[t]) for t in range(TILES)]
        return [pltpu.make_async_copy(b, a, sem.at[t]) if out else pltpu.make_async_copy(a, b, sem.at[t])
                for t, (a, b) in enumerate(pairs)]

    cot_load = pltpu.make_async_copy(cot_hbm, cot_v, in_sems.at[0])
    state_load = tiles(state_hbm, state_v, tile_sems.at[0])
    rest = tiles(diff_hbm, diff_v, tile_sems.at[1]) + [
        pltpu.make_async_copy(src, dst, in_sems.at[i + 1])
        for i, (src, dst) in enumerate(((vinv_hbm, vinv_v), (w_in_hbm, w_in_v), (w_out_hbm, w_out_v)))
    ]
    loads = [cot_load] + state_load + rest
    for load in loads:
        load.start()

    barrier = pltpu.get_barrier_semaphore()

    @pl.loop(1, LEVS)
    def _(j):
        pl.semaphore_signal(
            barrier, inc=1, device_id={"lev": lax.rem(me + j, LEVS), "hor": hor}, device_id_type=MESH
        )

    @pl.when(hor > 0)
    def _():
        pl.semaphore_signal(barrier, inc=1, device_id={"lev": me, "hor": hor - 1}, device_id_type=MESH)

    @pl.when(hor < last)
    def _():
        pl.semaphore_signal(barrier, inc=1, device_id={"lev": me, "hor": hor + 1}, device_id_type=MESH)

    def slot(r):
        depth = jnp.minimum(r, ROWS - 1 - r)
        return depth // 2, lax.rem(depth, 2) * 8 + (r >= ROWS // 2).astype(jnp.int32) * 4

    def put(buf, r, row):
        c, first = slot(r)
        for i in range(4):
            buf[c, first + i] = row[:, i * WIDE:(i + 1) * WIDE]

    def take(buf, r):
        c, first = slot(r)
        return jnp.concatenate([buf[c, first + i] for i in range(4)], axis=1).astype(F32)

    def across(ref, base, lo=0, hi=COLS):
        return jnp.concatenate(
            [ref[t, pl.ds(base, 8, stride=ROWS), :] for t in range(lo // 128, hi // 128)], axis=1
        )

    def both(ref, r):
        return jnp.concatenate([across(ref, r), across(ref, 128 + r)], axis=0)

    def doubled(ref, r, lo=0, hi=COLS):
        coef = across(ref, r, lo, hi)
        return jnp.concatenate([coef, coef], axis=0)

    cot_load.wait()
    for t in range(TILES):
        cot_f[t] = cot_v[:, t * 128:(t + 1) * 128].astype(F32)

    @pl.loop(0, ROWS)
    def _(r):
        put(s_cot, r, both(cot_f, r).astype(BF16))

    for c in range(CHUNKS):
        r_cot[c, me] = s_cot[c, me]

    for load in state_load:
        load.wait()

    for r in (0, ROWS - 1):
        grid_s[r + 1] = both(state_v, r)

    @pl.when(hor == 0)
    def _():
        grid_s[0] = jnp.zeros((16, COLS), F32)
        grid_w[0] = jnp.zeros((16, COLS), F32)

    @pl.when(hor == last)
    def _():
        grid_s[ROWS + 1] = jnp.zeros((16, COLS), F32)
        grid_w[ROWS + 1] = jnp.zeros((16, COLS), F32)

    pl.semaphore_wait(
        barrier, LEVS - 1 + (hor > 0).astype(jnp.int32) + (hor < last).astype(jnp.int32)
    )

    def edge(k, up):
        return pltpu.make_async_remote_copy(
            src_ref=s_edge.at[k, up], dst_ref=r_edge.at[k, up],
            send_sem=edge_sems.at[0, k, up], recv_sem=edge_sems.at[1, k, up],
            device_id={"lev": me, "hor": hor + 2 * up - 1}, device_id_type=MESH,
        )

    def swap_start(k, grid):
        @pl.when(hor > 0)
        def _():
            s_edge[k, 0] = grid[1].astype(BF16)
            edge(k, 0).start()

        @pl.when(hor < last)
        def _():
            s_edge[k, 1] = grid[ROWS].astype(BF16)
            edge(k, 1).start()

    def swap_wait(k, grid):
        @pl.when(hor > 0)
        def _():
            edge(k, 0).wait_send()
            edge(k, 1).wait_recv()
            grid[0] = r_edge[k, 1].astype(F32)

        @pl.when(hor < last)
        def _():
            edge(k, 1).wait_send()
            edge(k, 0).wait_recv()
            grid[ROWS + 1] = r_edge[k, 0].astype(F32)

    def spread(src, dst, sems, c):
        @pl.loop(1, LEVS)
        def _(j):
            peer = lax.rem(me + j, LEVS)
            pltpu.make_async_remote_copy(
                src_ref=src.at[c, peer], dst_ref=dst.at[c, me],
                send_sem=sems.at[0, c], recv_sem=sems.at[1, c],
                device_id={"lev": peer, "hor": hor}, device_id_type=MESH,
            ).start()

    def gathered(buf, sems, way, c):
        part = buf.at[c, pl.ds(0, LEVS - 1)]
        pltpu.make_async_copy(part, part, sems.at[way, c]).wait()

    swap_start(0, grid_s)
    for c in range(CHUNKS):
        spread(s_cot, r_cot, cot_sems, c)

    for load in rest:
        load.wait()

    @pl.loop(1, ROWS - 1)
    def _(r):
        grid_s[r + 1] = both(state_v, r)

    swap_wait(0, grid_s)

    @pl.loop(0, ROWS)
    def _(r):
        mid = grid_s[r + 1]
        around = grid_s[r] + grid_s[r + 2] + sides_of(mid) - 4.0 * mid
        put(s_state, r, (mid + doubled(diff_v, r) * around).astype(BF16))

    at_p = lax.broadcasted_iota(jnp.int32, (256, 256), 0)
    at_k = lax.broadcasted_iota(jnp.int32, (256, 256), 1)
    place = (at_p // 16) * 8 + (at_p % 16) // 8 * 128 + at_p % 8
    perm_t = (place == at_k).astype(F32).astype(BF16)
    w_in_p[...] = nt(w_in_v[...], perm_t).astype(BF16)
    w_in_t[...] = nt(perm_t, w_in_v[...]).astype(BF16)
    w_out_t[...] = nn(perm_t, w_out_v[...]).T.astype(BF16)
    eye = lax.broadcasted_iota(jnp.int32, (128, 128), 0) == lax.broadcasted_iota(jnp.int32, (128, 128), 1)
    parts = [jnp.zeros((256, 256), F32) for _ in range(2)]
    for f in range(2):
        exact = vinv_v[f]
        high = exact.astype(BF16)
        low = (exact - high.astype(F32)).astype(BF16)
        sel = perm_t[:, f * 128:(f + 1) * 128]
        for i, piece in enumerate((high, low)):
            parts[i] += nn(sel, nt(piece, sel).astype(BF16))
        diag = jnp.sum(jnp.where(eye, exact, 0.0), axis=1, keepdims=True)
        for src in range(LEVS):
            gain[src * 16 + f * 8:src * 16 + f * 8 + 8, :] = jnp.broadcast_to(
                diag[src * 8:src * 8 + 8], (8, 128)
            )
    for i in range(2):
        v_fwd[:, i * 256:(i + 1) * 256] = parts[i].astype(BF16)
    high_t = parts[0].T.astype(BF16)
    v_adj[:, 0:256] = high_t
    v_adj[:, 256:512] = high_t
    v_adj[:, 512:768] = parts[1].T.astype(BF16)

    steps = [(s_cot, r_cot, cot_sems, c) for c in range(CHUNKS)]
    steps += [(s_state, r_state, state_sems, c) for c in range(CHUNKS)]
    for k in range(CHUNKS - AHEAD):
        gathered(steps[k][1], steps[k][2], 1, steps[k][3])
    for k in range(CHUNKS, len(steps)):
        if k >= AHEAD:
            before = steps[k - AHEAD]
            gathered(before[1], before[2], 1, before[3])
        spread(*steps[k])
    done = len(steps) - AHEAD

    for c in range(CHUNKS):
        r_state[c, me] = s_state[c, me]

    def columns(c):
        diffused = r_state[c].reshape(256, WIDE)
        cot = r_cot[c].reshape(256, WIDE)
        solved = nn(v_fwd[...], jnp.concatenate([diffused, diffused], axis=0))
        inputs = solved.astype(BF16)
        level = cot.astype(F32)
        for h in range(4):
            hs = slice(h * 256, (h + 1) * 256)
            preact = nn(w_in_p[hs, :], inputs)
            hidden = nn(w_out_t[hs, :], cot)
            s = 0.5 + 0.5 * jnp.tanh(0.5 * preact)
            pre = (hidden * s * (1.0 + preact * (1.0 - s))).astype(BF16)
            level = level + nn(w_in_t[:, hs], pre)
        high = level.astype(BF16)
        low = (level - high.astype(F32)).astype(BF16)
        adjoint = nn(v_adj[...], jnp.concatenate([high, low, high], axis=0))
        delta = adjoint - gain[:, 0:1] * cot.astype(F32)
        s_adj[c] = delta.astype(BF16).reshape(LEVS, 16, WIDE)

    @pl.loop(0, CHUNKS)
    def _(c):
        @pl.when(c >= done)
        def _():
            gathered(r_cot, cot_sems, 1, c)

        @pl.when(c + CHUNKS >= done)
        def _():
            gathered(r_state, state_sems, 1, c)
        columns(c)
        spread(s_adj, r_adj, adj_sems, c)
        r_adj[c, me] = s_adj[c, me]

    scale = gain[pl.ds(pl.multiple_of(me * 16, 16), 16), 0:1]

    def stencil(r):
        mid = grid_w[r + 1]
        row = adj_v[r] + (grid_w[r] + grid_w[r + 2] + sides_of(mid) - 4.0 * mid)
        for t in range(TILES):
            out_v[t, pl.ds(r, 8, stride=ROWS), :] = row[0:8, t * 128:(t + 1) * 128]
            out_v[t, pl.ds(128 + r, 8, stride=ROWS), :] = row[8:16, t * 128:(t + 1) * 128]

    def mirrored(start, stop, one):
        @pl.loop(start, stop)
        def _(r):
            one(r)
            one(ROWS - 1 - r)

    def weigh(r):
        adj = take(r_adj, r) + scale * take(s_cot, r)
        adj_v[r] = adj
        grid_w[r + 1] = doubled(diff_v, r) * adj

    for c in range(CHUNKS):
        gathered(r_adj, adj_sems, 1, c)
        mirrored(2 * c, 2 * c + 2, weigh)
        if c == 0:
            swap_start(1, grid_w)
        if c == CHUNKS - 2:
            swap_wait(1, grid_w)
            mirrored(0, 1, stencil)
        mirrored(max(1, 2 * c - 1), 2 * c + (2 if c == CHUNKS - 1 else 1), stencil)

    stores = tiles(out_hbm, out_v, tile_sems.at[2], out=True)
    for store in stores:
        store.start()
    for c in range(CHUNKS):
        gathered(s_cot, cot_sems, 0, c)
        gathered(s_state, state_sems, 0, c)
        gathered(s_adj, adj_sems, 0, c)
    for store in stores:
        store.wait()


def body(state, cotangent, diffusion, vertical_inverse, w_in, w_out):
    dma = pltpu.SemaphoreType.DMA
    slabs = (CHUNKS, LEVS, 16, WIDE)
    out = pl.pallas_call(
        kernel,
        out_shape=pltpu.VMEM((256, COLS), F32),
        in_specs=[pl.BlockSpec(memory_space=pltpu.HBM)] * 6,
        out_specs=pl.BlockSpec(memory_space=pltpu.VMEM),
        scratch_shapes=[
            pltpu.VMEM((TILES, 256, 128), F32), pltpu.VMEM((256, COLS), BF16), pltpu.VMEM((TILES, 128, 128), F32),
            pltpu.VMEM((2, 128, 128), F32), pltpu.VMEM((HID, 256), BF16), pltpu.VMEM((256, HID), BF16),
            pltpu.VMEM((TILES, 256, 128), F32),
            pltpu.VMEM((TILES, 256, 128), F32), pltpu.VMEM((ROWS + 2, 16, COLS), F32),
            pltpu.VMEM((ROWS + 2, 16, COLS), F32), pltpu.VMEM((ROWS, 16, COLS), F32),
        ] + [pltpu.VMEM((2, 2, 16, COLS), BF16)] * 2 + [pltpu.VMEM(slabs, BF16)] * 6 + [
            pltpu.VMEM((HID, 256), BF16), pltpu.VMEM((256, HID), BF16), pltpu.VMEM((HID, 256), BF16),
            pltpu.VMEM((256, 512), BF16), pltpu.VMEM((256, 768), BF16), pltpu.VMEM((256, 128), F32),
            dma((4,)), dma((3, TILES)), dma((2, CHUNKS)), dma((2, CHUNKS)), dma((2, CHUNKS)), dma((2, 2, 2)),
        ],
        compiler_params=pltpu.CompilerParams(
            collective_id=0, has_side_effects=True, vmem_limit_bytes=44 << 20
        ),
    )(*[
        pltpu.with_memory_space_constraint(x, pltpu.HBM)
        for x in (state.reshape(256, COLS), cotangent.reshape(256, COLS), diffusion.reshape(128, COLS),
                  vertical_inverse, w_in, w_out)
    ])
    return out.reshape(2, 8, ROWS, COLS)


def solution(mesh):
    placed = (
        P(None, "lev", "hor", None),
        P(None, "lev", "hor", None),
        P("lev", "hor", None),
        P(),
        P(),
        P(),
    )
    return jax.shard_map(
        body, mesh=mesh, in_specs=placed, out_specs=P(None, "lev", "hor", None), check_vma=False
    )
```
